32 devices in a mesh: grid: 4 (over y, x), band: 8 (over z, core).
Axes of the slice: x: 2, y: 2, z: 4, core: 2. Of those that a mesh axis runs over, the one named last changes fastest.
Arguments:
- orbitals: float32 [160, 16, 64, 128], P('band', 'grid'), may hold values from -6 to 6
- occupation: float32 [160], P('band'), may hold values from 0.00625 to 0.05
- core_density: float32 [16, 64, 128], P('grid'), may hold values from 0.2 to 2
- local_potential: float32 [16, 64, 128], P('grid'), may hold values from -6 to 6
Outputs:
- applied: float32 [160, 16, 64, 128], P('band', 'grid')
The draws below stay inside these ranges and needn't reach their ends.
All inputs are finite; a program needn't handle non-finite values.
Results may differ from the reference program's by a relative error of at most 0.0001.
Values sent between devices are 32-bit elements; how exact they have to be, the bound alone decides.
A program may use at most 192 MiB of HBM per device.

```python
import math
import jax
import jax.numpy as jnp
from jax import lax

NY = 64
NZ = 128
BANDS = 160
NX = 16


def block_levels(key, shape, shards, low, high):
    loudness = 1.0
    for dim, parts in shards:
        draws = jax.random.uniform(jax.random.fold_in(jax.random.fold_in(key, 6), dim), (parts,), jnp.float32, low / len(shards), high / len(shards))
        loudness = loudness * jnp.repeat(jnp.exp(draws), shape[dim] // parts).reshape((-1,) + (1,) * (len(shape) - 1 - dim))
    return loudness


def normal_values(own_key, dims, scale, most, split=(), kind=jnp.bfloat16):
    drawn = jax.random.normal(own_key, dims, jnp.float32) * scale
    if len(split) > 0:
        drawn = block_levels(own_key, dims, split, -0.22, 0.18) * drawn
    return jnp.clip(drawn, min=-most, max=most).astype(kind)


def setup_inputs(seed: int = 0) -> dict:
    key_of = jax.random.split(jax.random.key(seed), 5)
    return {
        "orbitals": normal_values(key_of[0], (BANDS, NX, NY, NZ), 1.0, 6.0, ((0, 8), (1, 4)), jnp.float32),
        "occupation": jnp.clip(jnp.exp(math.log(0.05) - 2.0794415 * jax.random.uniform(key_of[1], (BANDS,), jnp.float32) ** block_levels(key_of[1], (BANDS,), ((0, 8),), -0.2, 0.2)), 0.00625, 0.05),
        "core_density": jnp.clip(jnp.exp(math.log(2.0) - 2.3025851 * jax.random.uniform(key_of[2], (NX, NY, NZ), jnp.float32) ** block_levels(key_of[2], (NX, NY, NZ), ((0, 4),), -0.2, 0.2)), 0.2, 2.0),
        "local_potential": normal_values(key_of[3], (NX, NY, NZ), 1.0, 6.0, ((0, 4),), jnp.float32),
    }


def derive(field, axis):
    ahead = jnp.roll(field, -1, axis) - jnp.roll(field, 1, axis)
    far = jnp.roll(field, -2, axis) - jnp.roll(field, 2, axis)
    return (8.0 * ahead - far) / 12.0


def pointwise(density, kinetic, local_potential):
    uniform = 2.871 * jnp.power(density, 5.0 / 3.0)
    ratio = kinetic / (kinetic + uniform)
    potential = local_potential - 0.7386 * jnp.power(density, 1.0 / 3.0) * (1.0 + 0.3 * ratio)
    weight = 1.0 + 0.4 * ratio
    return potential, weight


def reference(orbitals, occupation, core_density, local_potential):
    blocks = orbitals.reshape((BANDS // 8, 8) + orbitals.shape[1:])
    weights = occupation.reshape((BANDS // 8, 8))

    def accumulate(carry, item):
        block, occ = item
        occ4 = occ[:, None, None, None]
        squares = derive(block, 1) ** 2 + derive(block, 2) ** 2 + derive(block, 3) ** 2
        rho = carry[0] + jnp.sum(occ4 * block * block, axis=0)
        tau = carry[1] + 0.5 * jnp.sum(occ4 * squares, axis=0)
        return (rho, tau), None

    start = (jnp.zeros(core_density.shape, jnp.float32), jnp.zeros(core_density.shape, jnp.float32))
    (rho_sum, tau_sum), _ = lax.scan(accumulate, start, (blocks, weights))
    potential, weight = pointwise(core_density + rho_sum, tau_sum, local_potential)

    def apply_block(block):
        result = -0.5 * (derive(weight[None] * derive(block, 1), 1) + derive(weight[None] * derive(block, 2), 2) + derive(weight[None] * derive(block, 3), 3))
        return result + potential[None] * block

    applied = lax.map(apply_block, blocks)
    return applied.reshape(orbitals.shape)
```

```python
import functools

import jax
import jax.numpy as jnp
from jax import lax
from jax.experimental import pallas as pl
from jax.experimental.pallas import tpu as pltpu
from jax.sharding import PartitionSpec as P

MESH = pl.DeviceIdType.MESH
NEAR = 8.0 / 12.0
FAR = 1.0 / 12.0


def derive_lead(f):
    n = f.shape[0]

    def at(s):
        return jnp.concatenate([f[s % n :], f[: s % n]], axis=0)

    return NEAR * (at(1) - at(-1)) - FAR * (at(2) - at(-2))


def derive_tile(f, axis):
    n = f.shape[axis]
    ahead = pltpu.roll(f, n - 1, axis) - pltpu.roll(f, 1, axis)
    far = pltpu.roll(f, n - 2, axis) - pltpu.roll(f, 2, axis)
    return NEAR * ahead - FAR * far


def kernel(G, NB, CH, orb, occ, core, lpot, out,
           F, lt, lr, part, red, wp, lw, wl, dx, ret, gys, gzs,
           fs, fr, fo, ls, lrs, lo, ps, pr, ws, wr, vs, vr, vo, rs, rr, ro):
    bands, nx, ny, nz = orb.shape
    X = nx * G
    R = ny // G
    rc = R // CH
    px = X // NB
    npx = nx // px
    me = lax.axis_index("grid")
    bi = lax.axis_index("band")

    def gpeer(k):
        return lax.rem(me + k, G)

    def bpeer(k):
        return lax.rem(bi + k, NB)

    barrier = pltpu.get_barrier_semaphore()
    for k in range(1, G):
        pl.semaphore_signal(barrier, inc=1, device_id={"grid": gpeer(k)}, device_id_type=MESH)
    for k in range(1, NB):
        pl.semaphore_signal(barrier, inc=1, device_id={"band": bpeer(k)}, device_id_type=MESH)
    pl.semaphore_wait(barrier, G - 1 + NB - 1)

    def rows(dev, c):
        return pl.ds(pl.multiple_of(dev * R + c * rc, 8), rc)

    mine = pl.ds(me * nx, nx)
    sends = []

    def remote(src, dst, s, r, dev):
        copy = pltpu.make_async_remote_copy(
            src_ref=src, dst_ref=dst, send_sem=s, recv_sem=r, device_id=dev, device_id_type=MESH)
        copy.start()
        sends.append(copy)
        return copy

    def local(src, dst, s):
        copy = pltpu.make_async_copy(src, dst, s)
        copy.start()
        return copy

    def spread(c):
        got = [
            remote(orb.at[:, :, rows(gpeer(k), c), :], F.at[c, :, mine], fs.at[c, k], fr.at[c, k], {"grid": gpeer(k)})
            for k in range(1, G)
        ]
        return got, local(orb.at[:, :, rows(me, c), :], F.at[c, :, mine], fo.at[c])

    spreads = [spread(0)]

    first = (bi == 0).astype(jnp.float32)

    def sums_x(x, _):
        def body(b, carry):
            tau, rho = carry
            f = orb[b, x]
            gy = derive_tile(f, 0)
            gz = derive_tile(f, 1)
            gys[b, x] = gy
            gzs[b, x] = gz
            o = occ[b]
            return tau + o * (gy * gy + gz * gz), rho + o * (f * f)

        zero = jnp.zeros((ny, nz), jnp.float32)
        tau, rho = lax.fori_loop(0, bands, body, (zero, zero))
        lt[0, x] = 0.5 * tau
        lt[1, x] = rho + first * core[x]
        return 0

    lax.fori_loop(0, nx, sums_x, 0)

    def all_rows(dev):
        return pl.ds(pl.multiple_of(dev * R, 8), R)

    lgot = [
        remote(lt.at[:, :, all_rows(gpeer(k)), :], lr.at[:, mine], ls.at[k], lrs.at[k], {"grid": gpeer(k)})
        for k in range(1, G)
    ]
    lown = local(lt.at[:, :, all_rows(me), :], lr.at[:, mine], lo)
    for c in range(1, CH):
        spreads.append(spread(c))

    vgot, vown, rgot, rown = [], [], [], []
    for c in range(CH):
        got, own = spreads[c]
        if c == 0:
            lown.wait()
            for copy in lgot:
                copy.wait_recv()
        own.wait()
        for copy in got:
            copy.wait_recv()

        def taux_body(b, acc):
            g = derive_lead(F[c, b])
            return acc + (0.5 * occ[b]) * (g * g)

        taux = lax.fori_loop(0, bands, taux_body, jnp.zeros((X, rc, nz), jnp.float32))
        for j in range(NB):
            part[c, j, 0] = taux[j * px : (j + 1) * px] + lr[0, j * px : (j + 1) * px, c * rc : (c + 1) * rc]
            part[c, j, 1] = lr[1, j * px : (j + 1) * px, c * rc : (c + 1) * rc]
        pgot = [
            remote(part.at[c, bpeer(k)], red.at[c, k], ps.at[c, k], pr.at[c, k], {"band": bpeer(k)})
            for k in range(1, NB)
        ]
        total = part[c, bi]
        for k in range(1, NB):
            pgot[k - 1].wait_recv()
            total = total + red[c, k]
        kinetic = total[0]
        density = total[1]
        third = jnp.exp(jnp.log(density) * (1.0 / 3.0))
        uniform = 2.871 * (density * third * third)
        ratio = kinetic / (kinetic + uniform)
        wp[c, bi, 0] = 1.0 + 0.4 * ratio
        wp[c, bi, 1] = -0.7386 * third * (1.0 + 0.3 * ratio)
        wgot = [
            remote(wp.at[c, bi], wp.at[c, bi], ws.at[c, k], wr.at[c, k], {"band": bpeer(k)})
            for k in range(1, NB)
        ]
        for copy in wgot:
            copy.wait_recv()
        vgot.append([
            remote(wp.at[c, pl.ds(gpeer(k) * npx, npx)], lw.at[c, me], vs.at[c, k], vr.at[c, k], {"grid": gpeer(k)})
            for k in range(1, G)
        ])
        vown.append(local(wp.at[c, pl.ds(me * npx, npx)], lw.at[c, me], vo.at[c]))
        weight = jnp.concatenate([wp[c, j, 0] for j in range(NB)], axis=0)

        def dx_body(b, _):
            dx[c, b] = -0.5 * derive_lead(weight * derive_lead(F[c, b]))
            return 0

        lax.fori_loop(0, bands, dx_body, 0)
        rgot.append([
            remote(dx.at[c, :, pl.ds(gpeer(k) * nx, nx)], ret.at[c, me], rs.at[c, k], rr.at[c, k], {"grid": gpeer(k)})
            for k in range(1, G)
        ])
        rown.append(local(dx.at[c, :, mine], ret.at[c, me], ro.at[c]))

    for c in range(CH):
        vown[c].wait()
        for copy in vgot[c]:
            copy.wait_recv()
        for p in range(G):
            at = p * R + c * rc
            for j in range(npx):
                wl[0, j * px : (j + 1) * px, at : at + rc] = lw[c, p, j, 0]
                wl[1, j * px : (j + 1) * px, at : at + rc] = (
                    lw[c, p, j, 1] + lpot[j * px : (j + 1) * px, at : at + rc]
                )

    def apply_x(x, _):
        w = wl[0, x]
        v = wl[1, x]

        def body(b, _):
            div = derive_tile(w * gys[b, x], 0) + derive_tile(w * gzs[b, x], 1)
            out[b, x] = v * orb[b, x] - 0.5 * div
            return 0

        return lax.fori_loop(0, bands, body, 0)

    lax.fori_loop(0, nx, apply_x, 0)

    for c in range(CH):
        rown[c].wait()
        for copy in rgot[c]:
            copy.wait_recv()

        def add_body(b, _):
            for p in range(G):
                at = p * R + c * rc
                out[b, :, at : at + rc] = out[b, :, at : at + rc] + ret[c, p, b]
            return 0

        lax.fori_loop(0, bands, add_body, 0)
    for copy in sends:
        copy.wait_send()


def per_device(orbitals, occupation, core_density, local_potential):
    G = lax.axis_size("grid")
    NB = lax.axis_size("band")
    bands, nx, ny, nz = orbitals.shape
    X = nx * G
    R = ny // G
    CH = 2 if R % 16 == 0 else 1
    rc = R // CH
    px = X // NB
    npx = nx // px
    f32 = jnp.float32
    dma = pltpu.SemaphoreType.DMA
    vmem = pl.BlockSpec(memory_space=pltpu.VMEM)
    return pl.pallas_call(
        functools.partial(kernel, G, NB, CH),
        out_shape=jax.ShapeDtypeStruct(orbitals.shape, f32),
        in_specs=[vmem, pl.BlockSpec(memory_space=pltpu.SMEM), vmem, vmem],
        out_specs=vmem,
        scratch_shapes=[
            pltpu.VMEM((CH, bands, X, rc, nz), f32),
            pltpu.VMEM((2, nx, ny, nz), f32),
            pltpu.VMEM((2, X, R, nz), f32),
            pltpu.VMEM((CH, NB, 2, px, rc, nz), f32),
            pltpu.VMEM((CH, NB, 2, px, rc, nz), f32),
            pltpu.VMEM((CH, NB, 2, px, rc, nz), f32),
            pltpu.VMEM((CH, G, npx, 2, px, rc, nz), f32),
            pltpu.VMEM((2, nx, ny, nz), f32),
            pltpu.VMEM((CH, bands, X, rc, nz), f32),
            pltpu.VMEM((CH, G, bands, nx, rc, nz), f32),
            pltpu.VMEM((bands, nx, ny, nz), f32),
            pltpu.VMEM((bands, nx, ny, nz), f32),
            dma((CH, G)), dma((CH, G)), dma((CH,)),
            dma((G,)), dma((G,)), dma,
            dma((CH, NB)), dma((CH, NB)),
            dma((CH, NB)), dma((CH, NB)),
            dma((CH, G)), dma((CH, G)), dma((CH,)),
            dma((CH, G)), dma((CH, G)), dma((CH,)),
        ],
        compiler_params=pltpu.CompilerParams(
            collective_id=0, has_side_effects=True, vmem_limit_bytes=60 * 1024 * 1024
        ),
    )(orbitals, occupation, core_density, local_potential)


def solution(mesh):
    in_specs = (
        P("band", "grid", None, None),
        P("band"),
        P("grid", None, None),
        P("grid", None, None),
    )
    out_specs = P("band", "grid", None, None)
    return jax.shard_map(
        per_device, mesh=mesh, in_specs=in_specs, out_specs=out_specs, check_vma=False
    )
```

```python
import functools

import jax
import jax.numpy as jnp
from jax import lax
from jax.experimental import pallas as pl
from jax.experimental.pallas import tpu as pltpu
from jax.sharding import PartitionSpec as P

MESH = pl.DeviceIdType.MESH
NEAR = 8.0 / 12.0
FAR = 1.0 / 12.0


def derive_lead(f):
    n = f.shape[0]

    def at(s):
        return jnp.concatenate([f[s % n :], f[: s % n]], axis=0)

    return NEAR * (at(1) - at(-1)) - FAR * (at(2) - at(-2))


def derive_tile(f, axis):
    n = f.shape[axis]
    ahead = pltpu.roll(f, n - 1, axis) - pltpu.roll(f, 1, axis)
    far = pltpu.roll(f, n - 2, axis) - pltpu.roll(f, 2, axis)
    return NEAR * ahead - FAR * far


def partner(i, k, n):
    if n & (n - 1):
        return lax.rem(i + k, n)
    out, bit = 0, 1
    while bit < n:
        digit = lax.rem(lax.div(i, bit), 2)
        out = out + bit * (1 - digit if k & bit else digit)
        bit *= 2
    return out


def kernel(G, NB, CH, orb_hbm, occ_hbm, core_hbm, lpot_hbm, out,
           orb, occ, core, lpot, F, lt, lred, lsum, lyz, part, red, wv, wy, lw, wl, dx, ret, gys, gzs,
           os, fs, fr, fo, ls, lr, ms, mr, ml, ps, pr, ws, wr, vs, vr, vl, us, ur, rs, rr, ro):
    bands, nx, ny, nz = orb.shape
    X = nx * G
    R = ny // G
    rc = R // CH
    px = X // NB
    npx = nx // px
    me = lax.axis_index("grid")
    bi = lax.axis_index("band")
    tg, tb = lax.rem(bi, G), npx * me + lax.div(bi, G)
    sg, sb = lax.div(bi, npx), lax.rem(bi, npx) * G + me
    here = jnp.logical_and(tg == me, tb == bi)
    away = jnp.logical_not(here)

    def gpeer(k):
        return partner(me, k, G)

    def bpeer(k):
        return partner(bi, k, NB)

    barrier = pltpu.get_barrier_semaphore()
    for k in range(1, G):
        pl.semaphore_signal(barrier, inc=1, device_id={"grid": gpeer(k)}, device_id_type=MESH)
    for k in range(1, NB):
        pl.semaphore_signal(barrier, inc=1, device_id={"band": bpeer(k)}, device_id_type=MESH)

    @pl.when(away)
    def _():
        for g, b in ((tg, tb), (sg, sb)):
            pl.semaphore_signal(barrier, inc=1, device_id={"grid": g, "band": b}, device_id_type=MESH)

    sends = []

    def remote(src, dst, s, r, dev):
        copy = pltpu.make_async_remote_copy(
            src_ref=src, dst_ref=dst, send_sem=s, recv_sem=r, device_id=dev, device_id_type=MESH)
        copy.start()
        sends.append(copy)
        return copy

    def local(src, dst, s):
        copy = pltpu.make_async_copy(src, dst, s)
        copy.start()
        return copy

    def moved(src, dst, s, r, l, g, b):
        far = pltpu.make_async_remote_copy(
            src_ref=src, dst_ref=dst, send_sem=s, recv_sem=r, device_id={"grid": g, "band": b},
            device_id_type=MESH)
        near = pltpu.make_async_copy(src, dst, l)
        pl.when(away)(far.start)
        pl.when(here)(near.start)

        def wait():
            pl.when(away)(far.wait)
            pl.when(here)(near.wait)

        return wait

    loads = [
        local(src, dst, os.at[i])
        for i, (src, dst) in enumerate(((orb_hbm, orb), (occ_hbm, occ), (core_hbm, core), (lpot_hbm, lpot)))
    ]
    pl.when(away)(lambda: pl.semaphore_wait(barrier, G - 1 + NB - 1 + 2))
    pl.when(here)(lambda: pl.semaphore_wait(barrier, G - 1 + NB - 1))

    def rows(dev, c):
        return pl.ds(pl.multiple_of(dev * R + c * rc, 8), rc)

    mine = pl.ds(me * nx, nx)

    def spread(c):
        got = [
            remote(orb_hbm.at[:, :, rows(gpeer(k), c), :], F.at[c, :, mine], fs.at[c, k], fr.at[c, k], {"grid": gpeer(k)})
            for k in range(1, G)
        ]
        return got, local(orb_hbm.at[:, :, rows(me, c), :], F.at[c, :, mine], fo.at[c])

    spreads = [spread(0)]
    for copy in loads:
        copy.wait()

    first = (bi == 0).astype(jnp.float32)

    def sums_x(x, _):
        def body(b, carry):
            tau, rho = carry
            f = orb[b, x]
            gy = derive_tile(f, 0)
            gz = derive_tile(f, 1)
            gys[b, x] = gy
            gzs[b, x] = gz
            o = occ[b]
            return tau + o * (gy * gy + gz * gz), rho + o * (f * f)

        zero = jnp.zeros((ny, nz), jnp.float32)
        tau, rho = lax.fori_loop(0, bands, body, (zero, zero))
        lt[0, x] = 0.5 * tau
        lt[1, x] = rho + first * core[x]
        return 0

    lax.fori_loop(0, nx, sums_x, 0)

    def piece(m):
        return (pl.ds(lax.div(m, G) * px, px), pl.ds(pl.multiple_of(lax.rem(m, G) * R, 8), R))

    lgot = []
    for k in range(1, NB):
        xs, ys = piece(bpeer(k))
        lgot.append(remote(lt.at[:, xs, ys, :], lred.at[k], ls.at[k], lr.at[k], {"band": bpeer(k)}))
    xs, ys = piece(bi)
    total = lt[:, xs, ys, :]
    for k in range(1, NB):
        lgot[k - 1].wait_recv()
        total = total + lred[k]
    lsum[...] = total
    lmove = moved(lsum, lyz, ms, mr, ml, tg, tb)
    for c in range(1, CH):
        spreads.append(spread(c))

    ugot, rgot, rown = [], [], []

    def share(c, move):
        move()
        ugot.append([
            remote(lw.at[c, bi], lw.at[c, bi], us.at[c, k], ur.at[c, k], {"band": bpeer(k)})
            for k in range(1, NB)
        ])

    move = None
    for c in range(CH):
        got, own = spreads[c]
        own.wait()
        for copy in got:
            copy.wait_recv()

        def taux_body(b, acc):
            g = derive_lead(F[c, b])
            return acc + (0.5 * occ[b]) * (g * g)

        taux = lax.fori_loop(0, bands, taux_body, jnp.zeros((X, rc, nz), jnp.float32))
        for j in range(NB):
            part[c, j] = taux[j * px : (j + 1) * px]
        pgot = [
            remote(part.at[c, bpeer(k)], red.at[c, k], ps.at[c, k], pr.at[c, k], {"band": bpeer(k)})
            for k in range(1, NB)
        ]
        if c == 0:
            lmove()
        else:
            share(c - 1, move)
        kinetic = part[c, bi] + lyz[0, :, c * rc : (c + 1) * rc]
        density = lyz[1, :, c * rc : (c + 1) * rc]
        third = jnp.exp(jnp.log(density) * (1.0 / 3.0))
        uniform = 2.871 * (density * third * third)
        for k in range(1, NB):
            pgot[k - 1].wait_recv()
            kinetic = kinetic + red[c, k]
        ratio = kinetic / (kinetic + uniform)
        wy[c, bi] = 1.0 + 0.4 * ratio
        wgot = [
            remote(wy.at[c, bi], wy.at[c, bi], ws.at[c, k], wr.at[c, k], {"band": bpeer(k)})
            for k in range(1, NB)
        ]
        wv[c, 0] = 1.0 + 0.4 * ratio
        wv[c, 1] = -0.7386 * third * (1.0 + 0.3 * ratio)
        move = moved(wv.at[c], lw.at[c, sb], vs.at[c], vr.at[c], vl.at[c], sg, sb)
        for copy in wgot:
            copy.wait_recv()
        weight = jnp.concatenate([wy[c, j] for j in range(NB)], axis=0)

        def dx_body(b, _):
            dx[c, b] = -0.5 * derive_lead(weight * derive_lead(F[c, b]))
            return 0

        lax.fori_loop(0, bands, dx_body, 0)
        rgot.append([
            remote(dx.at[c, :, pl.ds(gpeer(k) * nx, nx)], ret.at[c, me], rs.at[c, k], rr.at[c, k], {"grid": gpeer(k)})
            for k in range(1, G)
        ])
        rown.append(local(dx.at[c, :, mine], ret.at[c, me], ro.at[c]))
    share(CH - 1, move)

    for c in range(CH):
        for copy in ugot[c]:
            copy.wait_recv()
        for m in range(NB):
            i, at = (m // G) * px, (m % G) * R + c * rc
            wl[0, i : i + px, at : at + rc] = lw[c, m, 0]
            wl[1, i : i + px, at : at + rc] = lw[c, m, 1] + lpot[i : i + px, at : at + rc]

    def apply_x(x, _):
        w = wl[0, x]
        v = wl[1, x]

        def body(b, _):
            div = derive_tile(w * gys[b, x], 0) + derive_tile(w * gzs[b, x], 1)
            out[b, x] = v * orb[b, x] - 0.5 * div
            return 0

        return lax.fori_loop(0, bands, body, 0)

    lax.fori_loop(0, nx, apply_x, 0)

    for c in range(CH):
        rown[c].wait()
        for copy in rgot[c]:
            copy.wait_recv()

        def add_body(b, _):
            for p in range(G):
                at = p * R + c * rc
                out[b, :, at : at + rc] = out[b, :, at : at + rc] + ret[c, p, b]
            return 0

        lax.fori_loop(0, bands, add_body, 0)
    for copy in sends:
        copy.wait_send()


def per_device(orbitals, occupation, core_density, local_potential):
    G = lax.axis_size("grid")
    NB = lax.axis_size("band")
    bands, nx, ny, nz = orbitals.shape
    X = nx * G
    R = ny // G
    CH = 2 if R % 16 == 0 else 1
    rc = R // CH
    px = X // NB
    f32 = jnp.float32
    dma = pltpu.SemaphoreType.DMA
    vmem = pl.BlockSpec(memory_space=pltpu.VMEM)
    return pl.pallas_call(
        functools.partial(kernel, G, NB, CH),
        out_shape=jax.ShapeDtypeStruct(orbitals.shape, f32),
        in_specs=[pl.BlockSpec(memory_space=pltpu.HBM)] * 4,
        out_specs=vmem,
        scratch_shapes=[
            pltpu.VMEM((bands, nx, ny, nz), f32),
            pltpu.SMEM((bands,), f32),
            pltpu.VMEM((nx, ny, nz), f32),
            pltpu.VMEM((nx, ny, nz), f32),
            pltpu.VMEM((CH, bands, X, rc, nz), f32),
            pltpu.VMEM((2, nx, ny, nz), f32),
            pltpu.VMEM((NB, 2, px, R, nz), f32),
            pltpu.VMEM((2, px, R, nz), f32),
            pltpu.VMEM((2, px, R, nz), f32),
            pltpu.VMEM((CH, NB, px, rc, nz), f32),
            pltpu.VMEM((CH, NB, px, rc, nz), f32),
            pltpu.VMEM((CH, 2, px, rc, nz), f32),
            pltpu.VMEM((CH, NB, px, rc, nz), f32),
            pltpu.VMEM((CH, NB, 2, px, rc, nz), f32),
            pltpu.VMEM((2, nx, ny, nz), f32),
            pltpu.VMEM((CH, bands, X, rc, nz), f32),
            pltpu.VMEM((CH, G, bands, nx, rc, nz), f32),
            pltpu.VMEM((bands, nx, ny, nz), f32),
            pltpu.VMEM((bands, nx, ny, nz), f32),
            dma((4,)), dma((CH, G)), dma((CH, G)), dma((CH,)),
            dma((NB,)), dma((NB,)), dma, dma, dma,
            dma((CH, NB)), dma((CH, NB)),
            dma((CH, NB)), dma((CH, NB)),
            dma((CH,)), dma((CH,)), dma((CH,)),
            dma((CH, NB)), dma((CH, NB)),
            dma((CH, G)), dma((CH, G)), dma((CH,)),
        ],
        compiler_params=pltpu.CompilerParams(
            collective_id=0, has_side_effects=True, vmem_limit_bytes=26 * 1024 * 1024
        ),
    )(*(
        pltpu.with_memory_space_constraint(a, pltpu.HBM)
        for a in (orbitals, occupation, core_density, local_potential)
    ))


def solution(mesh):
    in_specs = (
        P("band", "grid", None, None),
        P("band"),
        P("grid", None, None),
        P("grid", None, None),
    )
    out_specs = P("band", "grid", None, None)
    return jax.shard_map(
        per_device, mesh=mesh, in_specs=in_specs, out_specs=out_specs, check_vma=False
    )
```

```python
import functools

import jax
import jax.numpy as jnp
from jax import lax
from jax.experimental import pallas as pl
from jax.experimental.pallas import tpu as pltpu
from jax.sharding import PartitionSpec as P

MESH = pl.DeviceIdType.MESH
NEAR = 8.0 / 12.0
FAR = 1.0 / 12.0


def derive_lead(f):
    n = f.shape[0]

    def at(s):
        return jnp.concatenate([f[s % n :], f[: s % n]], axis=0)

    return NEAR * (at(1) - at(-1)) - FAR * (at(2) - at(-2))


def derive_tile(f, axis):
    n = f.shape[axis]
    ahead = pltpu.roll(f, n - 1, axis) - pltpu.roll(f, 1, axis)
    far = pltpu.roll(f, n - 2, axis) - pltpu.roll(f, 2, axis)
    return NEAR * ahead - FAR * far


def partner(i, k, n):
    if n & (n - 1):
        return lax.rem(i + k, n)
    out, bit = 0, 1
    while bit < n:
        digit = lax.rem(lax.div(i, bit), 2)
        out = out + bit * (1 - digit if k & bit else digit)
        bit *= 2
    return out


def kernel(G, NB, CH, orb_hbm, occ_hbm, core_hbm, lpot_hbm, out,
           orb, occ, core, lpot, F, lt, lred, lsum, lyz, part, red, wv, wy, lw, wl, dx, ret, gys, gzs,
           os, fs, fr, fo, ls, lr, ms, mr, ml, ps, pr, ws, wr, vs, vr, vl, us, ur, rs, rr, ro):
    bands, nx, ny, nz = orb.shape
    X = nx * G
    R = ny // G
    rc = R // CH
    px = X // NB
    npx = nx // px
    me = lax.axis_index("grid")
    bi = lax.axis_index("band")
    tg, tb = lax.rem(bi, G), npx * me + lax.div(bi, G)
    sg, sb = lax.div(bi, npx), lax.rem(bi, npx) * G + me
    here = jnp.logical_and(tg == me, tb == bi)
    away = jnp.logical_not(here)

    def gpeer(k):
        return partner(me, k, G)

    def bpeer(k):
        return partner(bi, k, NB)

    barrier = pltpu.get_barrier_semaphore()
    for k in range(1, G):
        pl.semaphore_signal(barrier, inc=1, device_id={"grid": gpeer(k)}, device_id_type=MESH)
    for k in range(1, NB):
        pl.semaphore_signal(barrier, inc=1, device_id={"band": bpeer(k)}, device_id_type=MESH)

    @pl.when(away)
    def _():
        for g, b in ((tg, tb), (sg, sb)):
            pl.semaphore_signal(barrier, inc=1, device_id={"grid": g, "band": b}, device_id_type=MESH)

    sends = []

    def remote(src, dst, s, r, dev):
        copy = pltpu.make_async_remote_copy(
            src_ref=src, dst_ref=dst, send_sem=s, recv_sem=r, device_id=dev, device_id_type=MESH)
        copy.start()
        sends.append(copy)
        return copy

    def local(src, dst, s):
        copy = pltpu.make_async_copy(src, dst, s)
        copy.start()
        return copy

    def moved(src, dst, s, r, l, g, b):
        far = pltpu.make_async_remote_copy(
            src_ref=src, dst_ref=dst, send_sem=s, recv_sem=r, device_id={"grid": g, "band": b},
            device_id_type=MESH)
        near = pltpu.make_async_copy(src, dst, l)
        pl.when(away)(far.start)
        pl.when(here)(near.start)

        def wait():
            pl.when(away)(far.wait)
            pl.when(here)(near.wait)

        return wait

    loads = [
        local(src, dst, os.at[i])
        for i, (src, dst) in enumerate(((orb_hbm, orb), (occ_hbm, occ), (core_hbm, core), (lpot_hbm, lpot)))
    ]
    pl.when(away)(lambda: pl.semaphore_wait(barrier, G - 1 + NB - 1 + 2))
    pl.when(here)(lambda: pl.semaphore_wait(barrier, G - 1 + NB - 1))

    def rows(dev, c):
        return pl.ds(pl.multiple_of(dev * R + c * rc, 8), rc)

    mine = pl.ds(me * nx, nx)

    def spread(c):
        got = [
            remote(orb_hbm.at[:, :, rows(gpeer(k), c), :], F.at[c, :, mine], fs.at[c, k], fr.at[c, k], {"grid": gpeer(k)})
            for k in range(1, G)
        ]
        return got, local(orb_hbm.at[:, :, rows(me, c), :], F.at[c, :, mine], fo.at[c])

    spreads = [spread(0)]
    for copy in loads:
        copy.wait()

    first = (bi == 0).astype(jnp.float32)

    def sums_x(x, _):
        def body(b, carry):
            tau, rho = carry
            f = orb[b, x]
            gy = derive_tile(f, 0)
            gz = derive_tile(f, 1)
            gys[b, x] = gy
            gzs[b, x] = gz
            o = occ[b]
            return tau + o * (gy * gy + gz * gz), rho + o * (f * f)

        zero = jnp.zeros((ny, nz), jnp.float32)
        tau, rho = lax.fori_loop(0, bands, body, (zero, zero), unroll=2)
        lt[0, x] = 0.5 * tau
        lt[1, x] = rho + first * core[x]
        return 0

    lax.fori_loop(0, nx, sums_x, 0)

    def piece(m):
        return (pl.ds(lax.div(m, G) * px, px), pl.ds(pl.multiple_of(lax.rem(m, G) * R, 8), R))

    lgot = []
    for k in range(1, NB):
        xs, ys = piece(bpeer(k))
        lgot.append(remote(lt.at[:, xs, ys, :], lred.at[k], ls.at[k], lr.at[k], {"band": bpeer(k)}))
    xs, ys = piece(bi)
    total = lt[:, xs, ys, :]
    for k in range(1, NB):
        lgot[k - 1].wait_recv()
        total = total + lred[k]
    lsum[...] = total
    lmove = moved(lsum, lyz, ms, mr, ml, tg, tb)
    for c in range(1, CH):
        spreads.append(spread(c))

    ugot, rgot, rown = [], [], []

    def share(c, move):
        move()
        ugot.append([
            remote(lw.at[c, bi], lw.at[c, bi], us.at[c, k], ur.at[c, k], {"band": bpeer(k)})
            for k in range(1, NB)
        ])

    move = None
    for c in range(CH):
        got, own = spreads[c]
        own.wait()
        for copy in got:
            copy.wait_recv()

        def taux_body(b, acc):
            g = derive_lead(F[c, b])
            return acc + (0.5 * occ[b]) * (g * g)

        taux = lax.fori_loop(0, bands, taux_body, jnp.zeros((X, rc, nz), jnp.float32))
        for j in range(NB):
            part[c, j] = taux[j * px : (j + 1) * px]
        pgot = [
            remote(part.at[c, bpeer(k)], red.at[c, k], ps.at[c, k], pr.at[c, k], {"band": bpeer(k)})
            for k in range(1, NB)
        ]
        if c == 0:
            lmove()
        else:
            share(c - 1, move)
        kinetic = part[c, bi] + lyz[0, :, c * rc : (c + 1) * rc]
        density = lyz[1, :, c * rc : (c + 1) * rc]
        third = jnp.exp(jnp.log(density) * (1.0 / 3.0))
        uniform = 2.871 * (density * third * third)
        for k in range(1, NB):
            pgot[k - 1].wait_recv()
            kinetic = kinetic + red[c, k]
        ratio = kinetic / (kinetic + uniform)
        wy[c, bi] = 1.0 + 0.4 * ratio
        wgot = [
            remote(wy.at[c, bi], wy.at[c, bi], ws.at[c, k], wr.at[c, k], {"band": bpeer(k)})
            for k in range(1, NB)
        ]
        wv[c, 0] = 1.0 + 0.4 * ratio
        wv[c, 1] = -0.7386 * third * (1.0 + 0.3 * ratio)
        move = moved(wv.at[c], lw.at[c, sb], vs.at[c], vr.at[c], vl.at[c], sg, sb)
        for copy in wgot:
            copy.wait_recv()
        weight = jnp.concatenate([wy[c, j] for j in range(NB)], axis=0)

        def dx_body(b, _):
            dx[c, b] = -0.5 * derive_lead(weight * derive_lead(F[c, b]))
            return 0

        lax.fori_loop(0, bands, dx_body, 0)
        rgot.append([
            remote(dx.at[c, :, pl.ds(gpeer(k) * nx, nx)], ret.at[c, me], rs.at[c, k], rr.at[c, k], {"grid": gpeer(k)})
            for k in range(1, G)
        ])
        rown.append(local(dx.at[c, :, mine], ret.at[c, me], ro.at[c]))
    share(CH - 1, move)

    for c in range(CH):
        for copy in ugot[c]:
            copy.wait_recv()
        for m in range(NB):
            i, at = (m // G) * px, (m % G) * R + c * rc
            wl[0, i : i + px, at : at + rc] = lw[c, m, 0]
            wl[1, i : i + px, at : at + rc] = lw[c, m, 1] + lpot[i : i + px, at : at + rc]

    def apply_x(x, _):
        w = wl[0, x]
        v = wl[1, x]

        def body(b, _):
            div = derive_tile(w * gys[b, x], 0) + derive_tile(w * gzs[b, x], 1)
            out[b, x] = v * orb[b, x] - 0.5 * div
            return 0

        return lax.fori_loop(0, bands, body, 0)

    lax.fori_loop(0, nx, apply_x, 0)

    for c in range(CH):
        rown[c].wait()
        for copy in rgot[c]:
            copy.wait_recv()

        def add_body(b, _):
            for p in range(G):
                at = p * R + c * rc
                out[b, :, at : at + rc] = out[b, :, at : at + rc] + ret[c, p, b]
            return 0

        lax.fori_loop(0, bands, add_body, 0)
    for copy in sends:
        copy.wait_send()


def per_device(orbitals, occupation, core_density, local_potential):
    G = lax.axis_size("grid")
    NB = lax.axis_size("band")
    bands, nx, ny, nz = orbitals.shape
    X = nx * G
    R = ny // G
    CH = 2 if R % 16 == 0 else 1
    rc = R // CH
    px = X // NB
    f32 = jnp.float32
    dma = pltpu.SemaphoreType.DMA
    vmem = pl.BlockSpec(memory_space=pltpu.VMEM)
    return pl.pallas_call(
        functools.partial(kernel, G, NB, CH),
        out_shape=jax.ShapeDtypeStruct(orbitals.shape, f32),
        in_specs=[pl.BlockSpec(memory_space=pltpu.HBM)] * 4,
        out_specs=vmem,
        scratch_shapes=[
            pltpu.VMEM((bands, nx, ny, nz), f32),
            pltpu.SMEM((bands,), f32),
            pltpu.VMEM((nx, ny, nz), f32),
            pltpu.VMEM((nx, ny, nz), f32),
            pltpu.VMEM((CH, bands, X, rc, nz), f32),
            pltpu.VMEM((2, nx, ny, nz), f32),
            pltpu.VMEM((NB, 2, px, R, nz), f32),
            pltpu.VMEM((2, px, R, nz), f32),
            pltpu.VMEM((2, px, R, nz), f32),
            pltpu.VMEM((CH, NB, px, rc, nz), f32),
            pltpu.VMEM((CH, NB, px, rc, nz), f32),
            pltpu.VMEM((CH, 2, px, rc, nz), f32),
            pltpu.VMEM((CH, NB, px, rc, nz), f32),
            pltpu.VMEM((CH, NB, 2, px, rc, nz), f32),
            pltpu.VMEM((2, nx, ny, nz), f32),
            pltpu.VMEM((CH, bands, X, rc, nz), f32),
            pltpu.VMEM((CH, G, bands, nx, rc, nz), f32),
            pltpu.VMEM((bands, nx, ny, nz), f32),
            pltpu.VMEM((bands, nx, ny, nz), f32),
            dma((4,)), dma((CH, G)), dma((CH, G)), dma((CH,)),
            dma((NB,)), dma((NB,)), dma, dma, dma,
            dma((CH, NB)), dma((CH, NB)),
            dma((CH, NB)), dma((CH, NB)),
            dma((CH,)), dma((CH,)), dma((CH,)),
            dma((CH, NB)), dma((CH, NB)),
            dma((CH, G)), dma((CH, G)), dma((CH,)),
        ],
        compiler_params=pltpu.CompilerParams(
            collective_id=0, has_side_effects=True, vmem_limit_bytes=26 * 1024 * 1024
        ),
    )(*(
        pltpu.with_memory_space_constraint(a, pltpu.HBM)
        for a in (orbitals, occupation, core_density, local_potential)
    ))


def solution(mesh):
    in_specs = (
        P("band", "grid", None, None),
        P("band"),
        P("grid", None, None),
        P("grid", None, None),
    )
    out_specs = P("band", "grid", None, None)
    return jax.shard_map(
        per_device, mesh=mesh, in_specs=in_specs, out_specs=out_specs, check_vma=False
    )
```
